512 devices in a mesh: tm: 16 (over z_hi, y), pipe: 2 (over core), dp: 16 (over x, z_lo).
Axes of the slice: x: 4, y: 4, z: 16 (z_hi: 4, z_lo: 4; z = z_hi * 4 + z_lo), core: 2. Of those that a mesh axis runs over, the one named last changes fastest.
Arguments:
- resid_in: float32 [2, 96, 1024, 1408], P('pipe', 'dp', 'tm'), may hold values from -6 to 6
- ln_gain: float32 [2, 1408], P('pipe'), may hold values from 0.5 to 1.5
- ln_bias: float32 [2, 1408], P('pipe'), may hold values from -2 to 2
- qkv_weight: bfloat16 [2, 1408, 2112], P('pipe', None, 'dp'), may hold values from -0.15625 to 0.15625
- q_bias: float32 [2, 704], P('pipe'), may hold values from -3 to 3
- v_bias: float32 [2, 704], P('pipe'), may hold values from -3 to 3
- out_weight: bfloat16 [2, 1408, 704], P('pipe', None, 'dp'), may hold values from -0.21875 to 0.21875
- out_bias: float32 [2, 1408], P('pipe'), may hold values from -2 to 2
- pattern: int32 [16, 96, 2], P('tm', 'dp'), may hold values from 0 to 14, all different within a row; in each aligned block of 6 rows (0 to 5, 6 to 11, ..., all dimensions but the last counted through in order) at most 2 rows name the same one
- drop_flags: int32 [2, 96], P('pipe', 'dp'), may hold values 0 or 1
Outputs:
- handoff: float32 [2, 96, 1024, 1408], P('pipe', 'dp', 'tm')
The draws below stay inside these ranges and needn't reach their ends.
Inputs may be any that keep to these rules, and one draw needn't show every extreme that they name: `pattern`: offset v of query block b names key block (b + 1 + v) mod 16; the 2 offsets of one query block and clip differ. Among the 6 clips of one dp index, one query block names one key block in at most 2 clips. `drop_flags`: 1 marks a layer dropped for a clip.
All inputs are finite; a program needn't handle non-finite values. No bound on the sum of `drop_flags` on one device may be relied on, other than what follows from the above.
Results may differ from the reference program's by a relative error of at most 0.0019.
Values may be sent and summed in bfloat16 or wider, within the bound.
No kernel may reach another device: no remote copies, remote signals or barrier semaphores. Data moves between devices by JAX's collectives and lax.ppermute only.
A program may use at most 64 MiB of HBM per device.

```python
import math
import jax
import jax.numpy as jnp
import numpy as np
from jax import lax

D = 1408
HEAD_DIM = 88
HEADS = 8
BLOCK = 64
TOP = 2
CLIPS_DEV = 6
HD = 704
CLIPS = 96
TOK_CLIP = 1024
MOST = 2
N_TM = 16


def place_ends(values, rng, least, high):
    longest = values.shape.index(max(values.shape))
    spots = []
    for shift in (0, 1):
        where = [jax.random.randint(jax.random.fold_in(rng, axis), (), 0, length) for axis, length in enumerate(values.shape)]
        where[longest] = (where[longest] + shift) % values.shape[longest]
        spots.append(tuple(where))
    return values.at[spots[0]].set(least).at[spots[1]].set(high)


def shard_levels(key, extent, pieces, smallest, top_value):
    factor_of, own = 1.0, jax.random.fold_in(key, 6)
    for dim, shards_of in pieces:
        draws = jnp.exp(jax.random.uniform(jax.random.fold_in(own, dim), (shards_of,), jnp.float32, smallest / len(pieces), top_value / len(pieces)))
        factor_of = factor_of * jnp.repeat(draws, extent[dim] // shards_of).reshape([-1 if axis == dim else 1 for axis in range(len(extent))])
    return factor_of


def deal_out(stream_key, own, number, rows, number_of, top, limit, lean):
    order = jax.random.permutation(stream_key, number_of)
    packed, usual = load_shares(number_of, rows * top, limit, lean, True), load_shares(number_of, rows * top, limit, lean, False)
    places = jnp.arange(number_of)

    def named(tallies, rotation):
        used = int((tallies > 0).sum())
        fixed = max(1, used // 4)
        moved = fixed + (places - fixed + rotation * (used - fixed)) % max(1, number_of - fixed)
        return jnp.zeros((number_of,), jnp.int32).at[order[jnp.where(places < fixed, places, moved)]].set(jnp.asarray(tallies, jnp.int32))

    tallies = jnp.where(number % 4 == 0, named(packed, number // 4), named(usual, number - number // 4 - 1))
    mixed = jax.random.permutation(jax.random.fold_in(own, 3), number_of)
    donor, receiver = mixed[0:number_of // 2 * 2:2], mixed[1:number_of // 2 * 2:2]
    slack = jnp.minimum(tallies[donor] - 1, limit - tallies[receiver]) // 2
    slack = jnp.where((donor == order[0]) | (receiver == order[0]) | (tallies[receiver] == 0), 0, jnp.maximum(slack, 0))
    moved = jax.random.randint(jax.random.fold_in(own, 4), (number_of // 2,), 0, 1 << 20) % (slack + 1)
    tallies = tallies.at[donor].add(-moved).at[receiver].add(moved)
    items = jnp.searchsorted(jnp.cumsum(tallies), jnp.arange(rows * top), side="right").astype(jnp.int32)
    listing = items.reshape(top, rows).T
    listing = listing[jax.random.permutation(jax.random.fold_in(own, 1), rows)]
    rotation = jax.random.randint(jax.random.fold_in(own, 2), (rows, 1), 0, top)
    return jnp.take_along_axis(listing, (jnp.arange(top)[None, :] + rotation) % top, axis=1)


def load_shares(amount, total, bound, lean, full):
    portions = [(1 << 20) // math.isqrt(grade ** lean) + 1 for grade in range(1, amount + 1)]
    largest = bound if full else min(bound, max(-(-total // amount), total * portions[0] // sum(portions)))
    least = 1 if total - largest >= amount - 1 else 0
    given, spare = [largest] + [least] * (amount - 1), total - largest - least * (amount - 1)
    while spare > 0:
        candidates = [i for i in range(1, amount) if given[i] < largest] or [i for i in range(1, amount) if given[i] < bound]
        mass, left = sum([portions[i] for i in candidates]), spare
        for i in candidates:
            extra = min(bound - given[i], max(1, left * portions[i] // mass), spare)
            given[i] = given[i] + extra
            spare = spare - extra
    return np.array(given)


def noise(key, dims, width, most, cuts=(), kind=jnp.bfloat16):
    entries = width * jax.random.normal(key, dims, jnp.float32)
    if cuts:
        entries = entries * shard_levels(key, dims, cuts, -0.22, 0.18)
    return jnp.clip(entries, -most, most).astype(kind)


def setup_inputs(seed: int = 0) -> dict:
    key_list = jax.random.split(jax.random.key(seed), 11)
    resid_in = noise(key_list[0], (2, CLIPS, TOK_CLIP, D), 1.0, 6.0, ((0, 2), (1, 16), (2, 16)), jnp.float32)
    ln_gain = jnp.clip(1.0 + 0.1 * jax.random.normal(key_list[1], (2, D), jnp.float32), 0.5, 1.5)
    ln_bias = noise(key_list[2], (2, D), 0.3, 2.0, ((0, 2),), jnp.float32)
    qkv_weight = noise(key_list[3], (2, D, 3 * HD), D ** -0.5, 0.15625, ((0, 2), (2, 16)))
    q_bias = noise(key_list[4], (2, HD), 0.5, 3.0, ((0, 2),), jnp.float32)
    v_bias = noise(key_list[5], (2, HD), 0.5, 3.0, ((0, 2),), jnp.float32)
    out_weight = noise(key_list[6], (2, D, HD), HD ** -0.5, 0.21875, ((0, 2), (2, 16)))
    out_bias = noise(key_list[7], (2, D), 0.3, 2.0, ((0, 2),), jnp.float32)
    pattern_keys = jax.random.split(jax.random.fold_in(key_list[8], 1), N_TM * CLIPS // CLIPS_DEV)
    pattern_turns = jax.random.permutation(jax.random.fold_in(key_list[8], 3), N_TM * CLIPS // CLIPS_DEV)
    pattern = jax.vmap(lambda own, number: deal_out(jax.random.fold_in(key_list[8], 2), own, number, CLIPS_DEV, N_TM - 1, TOP, MOST, 2))(pattern_keys, pattern_turns).reshape((N_TM, CLIPS, TOP))
    drop_flags = place_ends((jax.random.randint(key_list[9], (2, CLIPS), 0, 4) < 1).astype(jnp.int32), jax.random.fold_in(key_list[9], 1), 0, 1)
    return {"resid_in": resid_in, "ln_gain": ln_gain, "ln_bias": ln_bias, "qkv_weight": qkv_weight, "q_bias": q_bias, "v_bias": v_bias, "out_weight": out_weight, "out_bias": out_bias, "pattern": pattern, "drop_flags": drop_flags}


drop_rate = 0.25

def to_wide(narrow):
    return lax.optimization_barrier(narrow).astype(jnp.float32)

def attend_clip(clip_rows, pat_rows, dropped, ln_scale, ln_shift, w_qkv, query_bias, value_bias, w_out, output_bias):
    average = lax.optimization_barrier(jnp.mean(clip_rows, axis=1, keepdims=True))
    centred = clip_rows - average
    spread = lax.optimization_barrier(jnp.mean(centred * centred, axis=1, keepdims=True))
    normed = (centred * lax.rsqrt(spread + 1e-06) * ln_scale + ln_shift).astype(jnp.bfloat16)
    hidden = HEADS * HEAD_DIM
    projected = jnp.dot(normed, w_qkv, preferred_element_type=jnp.float32)
    zero_bias = jnp.zeros((hidden,), jnp.float32)
    bias_full = jnp.concatenate([query_bias, zero_bias, value_bias])
    projected = (projected + bias_full).astype(jnp.bfloat16)
    head_shape = (N_TM, BLOCK, HEADS, HEAD_DIM)
    queries = to_wide(projected[:, :hidden]).reshape(head_shape)
    key_rows = to_wide(projected[:, hidden:2 * hidden]).reshape(head_shape)
    value_rows = to_wide(projected[:, 2 * hidden:]).reshape(head_shape)
    blocks = jnp.arange(N_TM, dtype=jnp.int32)
    chosen = jnp.concatenate([blocks[:, None], (blocks[:, None] + 1 + pat_rows) % N_TM], axis=1).astype(jnp.int32)
    near_keys = key_rows[chosen].reshape(N_TM, (1 + TOP) * BLOCK, HEADS, HEAD_DIM)
    near_vals = value_rows[chosen].reshape(N_TM, (1 + TOP) * BLOCK, HEADS, HEAD_DIM)
    scores = jnp.einsum('bqhd,bkhd->bhqk', queries, near_keys) * HEAD_DIM ** (-0.5)
    weights = jnp.exp(scores)
    totals = lax.optimization_barrier(jnp.sum(weights, axis=3))
    rounded = to_wide(weights.astype(jnp.bfloat16))
    weighted = jnp.einsum('bhqk,bkhd->bqhd', rounded, near_vals)
    attended = (weighted / jnp.transpose(totals, (0, 2, 1))[..., None]).astype(jnp.bfloat16)
    attended = attended.reshape(N_TM * BLOCK, hidden)
    branch = jnp.dot(attended, w_out.T, preferred_element_type=jnp.float32) + output_bias
    survive = (1 - dropped).astype(jnp.float32)
    return clip_rows + survive * branch / (1.0 - drop_rate)

def reference(resid_in, ln_gain, ln_bias, qkv_weight, q_bias, v_bias, out_weight, out_bias, pattern, drop_flags):
    pattern_by_clip = jnp.transpose(pattern, (1, 0, 2))
    results = []
    for segment_index in range(2):

        def one_clip(items):
            clip_rows, pat_rows, dropped = items
            return attend_clip(clip_rows, pat_rows, dropped, ln_gain[segment_index], ln_bias[segment_index], qkv_weight[segment_index], q_bias[segment_index], v_bias[segment_index], out_weight[segment_index], out_bias[segment_index])
        results.append(lax.map(one_clip, (resid_in[segment_index], pattern_by_clip, drop_flags[segment_index])))
    return jnp.stack([results[1], results[0]])
```

```python
import functools

import jax
import jax.numpy as jnp
from jax import lax
from jax.experimental import pallas as pl
from jax.experimental.pallas import tpu as pltpu
from jax.sharding import PartitionSpec as P

HEAD_DIM = 88
DROP_RATE = 0.25
UNIT = 44
PAD = 48
BF = jnp.bfloat16
F32 = jnp.float32

Z_GROUPS = [[4 * zh + y for zh in range(4)] for y in range(4)]
Y_GROUPS = [[4 * zh + y for y in range(4)] for zh in range(4)]
PLANE_GROUPS = [
    [(4 * zh + y) * 16 + 4 * x + zl for x in range(4) for y in range(4)]
    for zh in range(4)
    for zl in range(4)
]


def params(limit=56 << 20):
    return pltpu.CompilerParams(vmem_limit_bytes=limit)


def norm_kernel(goal_ref, a_ref, b_ref, gain_ref, bias_ref, out_ref):
    z = pl.program_id(0)
    for k, src in enumerate((a_ref, b_ref)):
        rows = src[0]
        mean = jnp.mean(rows, axis=1, keepdims=True)
        centred = rows - mean
        spread = jnp.mean(centred * centred, axis=1, keepdims=True)
        out_ref[0, 64 * k : 64 * k + 64] = (
            centred * lax.rsqrt(spread + 1e-06) * gain_ref[...] + bias_ref[...]
        ).astype(BF)
    row = lax.broadcasted_iota(jnp.int32, (8, 1408), 0)
    tail = jnp.zeros((8, 1408), jnp.int32)
    for k in range(4):
        clip = z if k < 2 else 4 + z // 2
        tail = jnp.where(row == k, goal_ref[2 * clip + k % 2], tail)
    out_ref[0, 128:136] = tail.astype(F32).astype(BF)


def normalise(goal, resid, gain, bias):
    block = (1, 64, 1408)
    return pl.pallas_call(
        norm_kernel,
        grid_spec=pltpu.PrefetchScalarGridSpec(
            num_scalar_prefetch=1,
            grid=(4,),
            in_specs=[
                pl.BlockSpec(block, lambda z, s: (z, 0, 0)),
                pl.BlockSpec(block, lambda z, s: (4 + z // 2, 0, 0)),
                pl.BlockSpec((1, 1408), lambda z, s: (0, 0)),
                pl.BlockSpec((1, 1408), lambda z, s: (0, 0)),
            ],
            out_specs=pl.BlockSpec((1, 136, 1408), lambda z, s: (z, 0, 0)),
        ),
        out_shape=jax.ShapeDtypeStruct((4, 136, 1408), BF),
        compiler_params=params(),
        name="norm",
    )(goal, resid, resid, gain, bias)


def qkv_kernel(par_ref, x_ref, w_ref, bias_ref, out_ref, acc, xs):
    step = pl.program_id(0)
    par = par_ref[0]

    @pl.when(step == 0)
    def _():
        for src in range(4):
            for k in range(2):
                at = 256 * k + 64 * src
                xs[at : at + 64] = x_ref[src, 64 * k : 64 * k + 64]

    weights = w_ref[0, 0:3].reshape(576, 1408)
    bias = bias_ref[0].reshape(576, 1)
    got = lax.dot_general(
        weights, xs[...], (((1,), (1,)), ((), ())), preferred_element_type=F32
    )
    got = (got + bias).astype(BF)
    for y in range(3):
        for zl in range(4):
            at = (y * 4 + zl) * PAD
            acc[12 * step + 3 * zl + y] = got[at : at + PAD]

    @pl.when(step == 3)
    def _():
        meta = jnp.concatenate([x_ref[src, 128:136, 0:64].astype(F32) for src in range(4)], axis=1)
        meta = jnp.concatenate([meta, jnp.zeros_like(meta)], axis=0).astype(BF)
        for y in range(4):
            for j in range(2):
                for g in range(3):
                    for k in range(2):
                        row = j * 288 + g * 96 + k * PAD
                        out_ref[y, row : row + PAD, :] = acc[16 * g + 4 * y + 2 * j + k, :, 0:256]
            for g in range(3):
                for k in range(2):
                    row = 576 + g * 96 + k * PAD
                    out_ref[y, row : row + PAD, :] = acc[16 * g + 4 * y + 2 * par + k, :, 256:512]
            out_ref[y, 864:880, :] = meta


def project(par, x, w, bias):
    return pl.pallas_call(
        qkv_kernel,
        grid_spec=pltpu.PrefetchScalarGridSpec(
            num_scalar_prefetch=1,
            grid=(4,),
            in_specs=[
                pl.BlockSpec((4, 136, 1408), lambda i, s: (0, 0, 0)),
                pl.BlockSpec((1, 4, 4, PAD, 1408), lambda i, s: (i, 0, 0, 0, 0)),
                pl.BlockSpec((1, 3, 4, PAD, 1), lambda i, s: (i, 0, 0, 0, 0)),
            ],
            out_specs=pl.BlockSpec((4, 880, 256), lambda i, s: (0, 0, 0)),
            scratch_shapes=[pltpu.VMEM((48, PAD, 512), BF), pltpu.VMEM((512, 1408), BF)],
        ),
        out_shape=jax.ShapeDtypeStruct((4, 880, 256), BF),
        compiler_params=params(),
        name="qkv",
    )(par, x, w, bias)


def attend_kernel(r_ref, out_ref, ot):
    scale = HEAD_DIM**-0.5
    lane_block = lax.broadcasted_iota(jnp.int32, (1, 256), 1) // 64
    for j in range(3):
        base = 288 * j
        row = 864 + (0 if j < 2 else 2)
        keys = [r_ref[yk, base + 96 : base + 192, :].astype(F32).T.astype(BF) for yk in range(4)]
        for yq in range(4):
            meta = r_ref[yq, 864:880, :].astype(F32)
            first = meta[row - 864 : row - 863, :].astype(jnp.int32)
            second = meta[row - 863 : row - 862, :].astype(jnp.int32)
            own = lane_block * 4 + yq
            queries = r_ref[yq, base : base + 96, :]
            total = jnp.zeros((1, 256), F32)
            mixed = jnp.zeros((96, 256), F32)
            for yk in range(4):
                scores = jnp.dot(keys[yk], queries, preferred_element_type=F32) * scale
                parts = []
                for zk in range(4):
                    block = zk * 4 + yk
                    seen = (first == block) | (second == block) | (own == block)
                    shift = jnp.where(seen, 0.0, -1e30)
                    parts.append(jnp.exp(scores[64 * zk : 64 * zk + 64, :] + shift))
                weights = jnp.concatenate(parts, axis=0)
                total = total + jnp.sum(weights, axis=0, keepdims=True)
                mixed = mixed + jnp.dot(
                    r_ref[yk, base + 192 : base + 288, :],
                    weights.astype(BF),
                    preferred_element_type=F32,
                )
            ot[j * 96 : j * 96 + 96, yq * 256 : yq * 256 + 256] = (mixed / total).astype(BF)
    for yq in range(4):
        for half in range(2):
            at = yq * 256 + half * 128
            low = ot[0:144, at : at + 128]
            high = ot[144:288, at : at + 128]
            out_ref[4 * (2 * half) + yq] = jnp.concatenate([low[:, :64], high[:, :64]], axis=1)
            out_ref[4 * (2 * half + 1) + yq] = jnp.concatenate([low[:, 64:], high[:, 64:]], axis=1)


def attend(r):
    return pl.pallas_call(
        attend_kernel,
        out_shape=jax.ShapeDtypeStruct((16, 144, 128), BF),
        in_specs=[pl.BlockSpec(memory_space=pltpu.VMEM)],
        out_specs=pl.BlockSpec(memory_space=pltpu.VMEM),
        scratch_shapes=[pltpu.VMEM((288, 1024), BF)],
        compiler_params=params(),
        name="attend",
    )(r)


def clip_rows(r_ref, clip):
    pieces = []
    for y in range(4):
        if clip < 4:
            t = 4 * clip + y
            pieces += [r_ref[t, :, 0:64], r_ref[t, 0:48, 64:128]]
        else:
            for odd in range(2):
                t = 4 * (2 * (clip - 4) + odd) + y
                pieces.append(r_ref[t, 48:144, 64:128])
    return jnp.concatenate(pieces, axis=0)


def out_kernel(keep_ref, r_ref, w_ref, resid_ref, bias_ref, out_ref):
    weights = w_ref[:, 0].reshape(768, 1408)
    for pair in range(3):
        rows = jnp.concatenate([clip_rows(r_ref, 2 * pair), clip_rows(r_ref, 2 * pair + 1)], axis=1)
        rows = rows.astype(F32).T.astype(BF)
        branch = jnp.dot(rows, weights, preferred_element_type=F32) + bias_ref[...]
        for k in range(2):
            clip = 2 * pair + k
            out_ref[clip] = resid_ref[clip] + branch[64 * k : 64 * k + 64] * keep_ref[clip]


def finish(keep, r, w, resid, bias):
    return pl.pallas_call(
        out_kernel,
        grid_spec=pltpu.PrefetchScalarGridSpec(
            num_scalar_prefetch=1,
            grid=(1,),
            in_specs=[
                pl.BlockSpec((16, 144, 128), lambda i, s: (0, 0, 0)),
                pl.BlockSpec((4, 1, 4, PAD, 1408), lambda i, s: (0, 3, 0, 0, 0)),
                pl.BlockSpec((6, 64, 1408), lambda i, s: (0, 0, 0)),
                pl.BlockSpec((1, 1408), lambda i, s: (0, 0)),
            ],
            out_specs=pl.BlockSpec((6, 64, 1408), lambda i, s: (0, 0, 0)),
        ),
        out_shape=jax.ShapeDtypeStruct((6, 64, 1408), F32),
        compiler_params=params(),
        name="finish",
    )(keep, r, w, resid, bias)


def z_exchange(x):
    return lax.all_to_all(x, "tm", 0, 0, axis_index_groups=Z_GROUPS, tiled=True)


def ring_perm(kind, by):
    pairs = []
    for z in range(16):
        for y in range(4):
            for x in range(4):
                to = {
                    "x": (z, y, (x + by) % 4),
                    "y": (z, (y + by) % 4, x),
                    "z": ((z + by) % 16, y, x),
                }[kind]
                flat = [(4 * (c // 4) + b) * 16 + 4 * a + c % 4 for c, b, a in ((z, y, x), to)]
                pairs.append(tuple(flat))
    return pairs


def shift(v, kind, by):
    return lax.ppermute(v, ("tm", "dp"), ring_perm(kind, by))


def in_order(rel, at):
    return lax.dynamic_slice_in_dim(jnp.concatenate([rel, rel]), 4 - at, 4, axis=0)


def gather_weights(qkv_weight, out_weight, y, zl):
    rows = jnp.concatenate([qkv_weight[0].T, out_weight[0].T], axis=0)
    quarter = lax.dynamic_slice(rows, (UNIT * y, 0), (UNIT, 1408))
    quarter = jnp.pad(quarter, ((0, PAD - UNIT), (0, 0)))
    rel = [quarter] + [shift(quarter, "z", by) for by in (-1, -2, 1)]
    line = in_order(jnp.stack(rel), zl)
    plane = lax.all_gather(line, ("tm", "dp"), axis=0, axis_index_groups=PLANE_GROUPS)
    return plane.reshape(4, 4, 4, PAD, 1408)


def body(
    resid_in, ln_gain, ln_bias, qkv_weight, q_bias, v_bias, out_weight, out_bias, pattern, drop_flags
):
    me = lax.axis_index("tm")
    zh, y = me // 4, me % 4
    resid = resid_in[0]
    zl = lax.axis_index("dp") % 4
    weights = gather_weights(qkv_weight, out_weight, y, zl)
    goal = ((me + 1 + pattern[0]) % 16).astype(jnp.int32).reshape(12)
    rows = z_exchange(normalise(goal, resid, ln_gain, ln_bias))
    bias = jnp.concatenate([q_bias[0], jnp.zeros((704,), F32), v_bias[0]])
    bias = jnp.pad(bias.reshape(4, 4, 3, UNIT), ((0, 0), (0, 0), (0, 0), (0, PAD - UNIT)))
    bias = bias.transpose(0, 2, 1, 3)[..., None]
    par = (zh % 2).astype(jnp.int32).reshape(1)
    packed = project(par, rows, weights, bias)
    heads = lax.all_to_all(packed, "tm", 0, 0, axis_index_groups=Y_GROUPS, tiled=True)
    mixed = attend(heads)
    home = lax.all_to_all(mixed, "tm", 0, 0, tiled=True)
    keep = (1 - drop_flags[0]).astype(F32) / (1.0 - DROP_RATE)
    updated = finish(keep, home, weights, resid, out_bias)
    received = lax.ppermute(updated, "pipe", [(0, 1), (1, 0)])
    return received[None]


def solution(mesh):
    return jax.shard_map(
        body,
        mesh=mesh,
        in_specs=(
            P("pipe", "dp", "tm", None),
            P("pipe", None),
            P("pipe", None),
            P("pipe", None, "dp"),
            P("pipe", None),
            P("pipe", None),
            P("pipe", None, "dp"),
            P("pipe", None),
            P("tm", "dp", None),
            P("pipe", "dp"),
        ),
        out_specs=P("pipe", "dp", "tm", None),
        check_vma=False,
    )
```

```python
import functools

import jax
import jax.numpy as jnp
from jax import lax
from jax.experimental import pallas as pl
from jax.experimental.pallas import tpu as pltpu
from jax.sharding import PartitionSpec as P

HEAD_DIM = 88
DROP_RATE = 0.25
UNIT = 44
PAD = 48
BF = jnp.bfloat16
F32 = jnp.float32

Z_GROUPS = [[4 * zh + y for zh in range(4)] for y in range(4)]
Y_GROUPS = [[4 * zh + y for y in range(4)] for zh in range(4)]
PLANE_GROUPS = [
    [(4 * zh + y) * 16 + 4 * x + zl for x in range(4) for y in range(4)]
    for zh in range(4)
    for zl in range(4)
]


def params(limit=56 << 20):
    return pltpu.CompilerParams(vmem_limit_bytes=limit)


def norm_kernel(goal_ref, a_ref, b_ref, gain_ref, bias_ref, out_ref):
    z = pl.program_id(0)
    for k, src in enumerate((a_ref, b_ref)):
        rows = src[0]
        mean = jnp.mean(rows, axis=1, keepdims=True)
        centred = rows - mean
        spread = jnp.mean(centred * centred, axis=1, keepdims=True)
        out_ref[0, 64 * k : 64 * k + 64] = (
            centred * lax.rsqrt(spread + 1e-06) * gain_ref[...] + bias_ref[...]
        ).astype(BF)
    row = lax.broadcasted_iota(jnp.int32, (8, 1408), 0)
    tail = jnp.zeros((8, 1408), jnp.int32)
    for k in range(4):
        clip = z if k < 2 else 4 + z // 2
        tail = jnp.where(row == k, goal_ref[2 * clip + k % 2], tail)
    out_ref[0, 128:136] = tail.astype(F32).astype(BF)


def normalise(goal, resid, gain, bias):
    block = (1, 64, 1408)
    return pl.pallas_call(
        norm_kernel,
        grid_spec=pltpu.PrefetchScalarGridSpec(
            num_scalar_prefetch=1,
            grid=(4,),
            in_specs=[
                pl.BlockSpec(block, lambda z, s: (z, 0, 0)),
                pl.BlockSpec(block, lambda z, s: (4 + z // 2, 0, 0)),
                pl.BlockSpec((1, 1408), lambda z, s: (0, 0)),
                pl.BlockSpec((1, 1408), lambda z, s: (0, 0)),
            ],
            out_specs=pl.BlockSpec((1, 136, 1408), lambda z, s: (z, 0, 0)),
        ),
        out_shape=jax.ShapeDtypeStruct((4, 136, 1408), BF),
        compiler_params=params(),
        name="norm",
    )(goal, resid, resid, gain, bias)


VM = pl.BlockSpec(memory_space=pltpu.VMEM)
SM = pl.BlockSpec(memory_space=pltpu.SMEM)
PARTS = ((0, 0, 4), (1, 0, 4), (3, 0, 4), (2, 0, 2), (2, 2, 2))


def qkv_kernel(pos_ref, x_ref, own, after, before, low, high, c_ref, bias_ref, out_ref, acc, xs):
    step = pl.program_id(0)
    y, par = pos_ref[0], pos_ref[2]

    @pl.when(step == 0)
    def _():
        for src in range(4):
            for k in range(2):
                at = 256 * k + 64 * src
                xs[at : at + 64] = x_ref[src, 64 * k : 64 * k + 64]

    def piece(weights, bias, place):
        got = lax.dot_general(
            weights, xs[...], (((1,), (1,)), ((), ())), preferred_element_type=F32
        )
        got = (got + bias).astype(BF)
        for u in range(weights.shape[0] // PAD):
            acc[place(u)] = got[PAD * u : PAD * u + PAD]

    piece(
        c_ref[0, 0:3].reshape(6 * PAD, 1408),
        bias_ref[0:3, step, 2:4].reshape(6 * PAD, 1),
        lambda u: 3 * (4 * step + 2 + u % 2) + u // 2,
    )
    for at, (w_ref, (r, x0, nx)) in enumerate(zip((own, after, before, low, high), PARTS)):
        ys = (y + r) % 4

        @pl.when((step == min(at, 3)) & (ys < 3))
        def _():
            piece(
                w_ref[...].reshape(nx * 2 * PAD, 1408),
                bias_ref[ys, x0 : x0 + nx, 0:2].reshape(nx * 2 * PAD, 1),
                lambda u: 3 * (4 * (x0 + u // 2) + u % 2) + ys,
            )

    @pl.when(step == 3)
    def _():
        meta = jnp.concatenate([x_ref[src, 128:136, 0:64].astype(F32) for src in range(4)], axis=1)
        meta = jnp.concatenate([meta, jnp.zeros_like(meta)], axis=0).astype(BF)
        for y in range(4):
            for j in range(2):
                for g in range(3):
                    for k in range(2):
                        row = j * 288 + g * 96 + k * PAD
                        out_ref[y, row : row + PAD, :] = acc[16 * g + 4 * y + 2 * j + k, :, 0:256]
            for g in range(3):
                for k in range(2):
                    row = 576 + g * 96 + k * PAD
                    out_ref[y, row : row + PAD, :] = acc[16 * g + 4 * y + 2 * par + k, :, 256:512]
            out_ref[y, 864:880, :] = meta


def fixed(shape):
    return pl.BlockSpec(shape, lambda i, s: (0,) * len(shape))


def project(pos, x, parts, c, bias):
    return pl.pallas_call(
        qkv_kernel,
        grid_spec=pltpu.PrefetchScalarGridSpec(
            num_scalar_prefetch=1,
            grid=(4,),
            in_specs=[fixed((4, 136, 1408))]
            + [fixed((nx, 2, PAD, 1408)) for _, _, nx in PARTS]
            + [
                pl.BlockSpec((1, 4, 2, PAD, 1408), lambda i, s: (i, 0, 0, 0, 0)),
                fixed((4, 4, 4, PAD, 1)),
            ],
            out_specs=fixed((4, 880, 256)),
            scratch_shapes=[pltpu.VMEM((48, PAD, 512), BF), pltpu.VMEM((512, 1408), BF)],
        ),
        out_shape=jax.ShapeDtypeStruct((4, 880, 256), BF),
        compiler_params=params(),
        name="qkv",
    )(pos, x, *parts, c, bias)


def collect_kernel(pos_ref, *refs):
    w_refs, c_ref, out_ref = refs[:5], refs[5], refs[6]
    for w_ref, (r, x0, nx) in zip(w_refs, PARTS):

        @pl.when((pos_ref[0] + r) % 4 == 3)
        def _():
            out_ref[x0 : x0 + nx, 0:2] = w_ref[...]

    out_ref[:, 2:4] = c_ref[:, 0]


def collect(pos, parts, c):
    return pl.pallas_call(
        collect_kernel,
        grid_spec=pltpu.PrefetchScalarGridSpec(
            num_scalar_prefetch=1,
            grid=(1,),
            in_specs=[fixed((nx, 2, PAD, 1408)) for _, _, nx in PARTS]
            + [pl.BlockSpec((4, 1, 2, PAD, 1408), lambda i, s: (0, 3, 0, 0, 0))],
            out_specs=fixed((4, 4, PAD, 1408)),
        ),
        out_shape=jax.ShapeDtypeStruct((4, 4, PAD, 1408), BF),
        compiler_params=params(),
        name="collect",
    )(pos, *parts, c)


def order_kernel(pos_ref, own, after, before, low, high, out_ref):
    at = pos_ref[1]
    out_ref[at] = own[...]
    out_ref[(at + 1) % 4] = after[...]
    out_ref[(at + 3) % 4] = before[...]
    out_ref[(at + 2) % 4, 0:1] = low[...]
    out_ref[(at + 2) % 4, 1:2] = high[...]


def order(pos, parts):
    return pl.pallas_call(
        order_kernel,
        in_specs=[SM] + [VM] * 5,
        out_specs=VM,
        out_shape=jax.ShapeDtypeStruct((4, 2, PAD, 1408), BF),
        compiler_params=params(),
        name="order",
    )(pos, *parts)


def attend_kernel(r_ref, out_ref, ot):
    scale = HEAD_DIM**-0.5
    lane_block = lax.broadcasted_iota(jnp.int32, (1, 256), 1) // 64
    for j in range(3):
        base = 288 * j
        row = 864 + (0 if j < 2 else 2)
        keys = [r_ref[yk, base + 96 : base + 192, :].astype(F32).T.astype(BF) for yk in range(4)]
        for yq in range(4):
            meta = r_ref[yq, 864:880, :].astype(F32)
            first = meta[row - 864 : row - 863, :].astype(jnp.int32)
            second = meta[row - 863 : row - 862, :].astype(jnp.int32)
            own = lane_block * 4 + yq
            queries = r_ref[yq, base : base + 96, :]
            total = jnp.zeros((1, 256), F32)
            mixed = jnp.zeros((96, 256), F32)
            for yk in range(4):
                scores = jnp.dot(keys[yk], queries, preferred_element_type=F32) * scale
                parts = []
                for zk in range(4):
                    block = zk * 4 + yk
                    seen = (first == block) | (second == block) | (own == block)
                    shift = jnp.where(seen, 0.0, -1e30)
                    parts.append(jnp.exp(scores[64 * zk : 64 * zk + 64, :] + shift))
                weights = jnp.concatenate(parts, axis=0)
                total = total + jnp.sum(weights, axis=0, keepdims=True)
                mixed = mixed + jnp.dot(
                    r_ref[yk, base + 192 : base + 288, :],
                    weights.astype(BF),
                    preferred_element_type=F32,
                )
            ot[j * 96 : j * 96 + 96, yq * 256 : yq * 256 + 256] = (mixed / total).astype(BF)
    for yq in range(4):
        for half in range(2):
            at = yq * 256 + half * 128
            low = ot[0:144, at : at + 128]
            high = ot[144:288, at : at + 128]
            out_ref[4 * (2 * half) + yq] = jnp.concatenate([low[:, :64], high[:, :64]], axis=1)
            out_ref[4 * (2 * half + 1) + yq] = jnp.concatenate([low[:, 64:], high[:, 64:]], axis=1)


def attend(r):
    return pl.pallas_call(
        attend_kernel,
        out_shape=jax.ShapeDtypeStruct((16, 144, 128), BF),
        in_specs=[pl.BlockSpec(memory_space=pltpu.VMEM)],
        out_specs=pl.BlockSpec(memory_space=pltpu.VMEM),
        scratch_shapes=[pltpu.VMEM((288, 1024), BF)],
        compiler_params=params(),
        name="attend",
    )(r)


def clip_rows(r_ref, clip):
    pieces = []
    for y in range(4):
        if clip < 4:
            t = 4 * clip + y
            pieces += [r_ref[t, :, 0:64], r_ref[t, 0:48, 64:128]]
        else:
            for odd in range(2):
                t = 4 * (2 * (clip - 4) + odd) + y
                pieces.append(r_ref[t, 48:144, 64:128])
    return jnp.concatenate(pieces, axis=0)


def out_kernel(keep_ref, r_ref, w_ref, resid_ref, bias_ref, out_ref):
    weights = w_ref[...].reshape(768, 1408)
    for pair in range(3):
        rows = jnp.concatenate([clip_rows(r_ref, 2 * pair), clip_rows(r_ref, 2 * pair + 1)], axis=1)
        rows = rows.astype(F32).T.astype(BF)
        branch = jnp.dot(rows, weights, preferred_element_type=F32) + bias_ref[...]
        for k in range(2):
            clip = 2 * pair + k
            out_ref[clip] = resid_ref[clip] + branch[64 * k : 64 * k + 64] * keep_ref[clip]


def finish(keep, r, w, resid, bias):
    return pl.pallas_call(
        out_kernel,
        grid_spec=pltpu.PrefetchScalarGridSpec(
            num_scalar_prefetch=1,
            grid=(1,),
            in_specs=[
                pl.BlockSpec((16, 144, 128), lambda i, s: (0, 0, 0)),
                pl.BlockSpec((4, 4, PAD, 1408), lambda i, s: (0, 0, 0, 0)),
                pl.BlockSpec((6, 64, 1408), lambda i, s: (0, 0, 0)),
                pl.BlockSpec((1, 1408), lambda i, s: (0, 0)),
            ],
            out_specs=pl.BlockSpec((6, 64, 1408), lambda i, s: (0, 0, 0)),
        ),
        out_shape=jax.ShapeDtypeStruct((6, 64, 1408), F32),
        compiler_params=params(),
        name="finish",
    )(keep, r, w, resid, bias)


def z_exchange(x):
    return lax.all_to_all(x, "tm", 0, 0, axis_index_groups=Z_GROUPS, tiled=True)


def ring_perm(kind, by):
    pairs = []
    for z in range(16):
        for y in range(4):
            for x in range(4):
                to = {
                    "x": (z, y, (x + by) % 4),
                    "y": (z, (y + by) % 4, x),
                    "z": ((z + by) % 16, y, x),
                }[kind]
                flat = [(4 * (c // 4) + b) * 16 + 4 * a + c % 4 for c, b, a in ((z, y, x), to)]
                pairs.append(tuple(flat))
    return pairs


def shift(v, kind, by):
    return lax.ppermute(v, ("tm", "dp"), ring_perm(kind, by))


def in_order(rel, at):
    return lax.dynamic_slice_in_dim(jnp.concatenate([rel, rel]), 4 - at, 4, axis=0)


def ring(v, kind):
    half = v.shape[0] // 2
    before = shift(v, kind, 1)
    after = shift(v, kind, -1)
    far_low = shift(before[:half], kind, 1)
    far_high = shift(after[half:], kind, -1)
    return v, after, before, far_low, far_high


def gather_weights(qkv_weight, out_weight, pos, y, zl, tie):
    rows = jnp.concatenate([qkv_weight[0].T, out_weight[0].T], axis=0)
    quarter = lax.dynamic_slice(rows, (UNIT * y, 0), (UNIT, 1408))
    quarter = jnp.pad(quarter, ((0, PAD - UNIT), (0, 0)))
    rel = [quarter] + [shift(quarter, "z", by) for by in (-1, -2, 1)]
    line = in_order(jnp.stack(rel), zl)
    plane = lax.all_gather(line[2:], ("tm", "dp"), axis=0, axis_index_groups=PLANE_GROUPS)
    first, tie = lax.optimization_barrier((line[:2], tie))
    parts = ring(order(pos, ring(first, "x")), "y")
    return parts, plane.reshape(4, 4, 2, PAD, 1408), tie


def other(v):
    return lax.ppermute(v, "pipe", [(0, 1), (1, 0)])


def body(
    resid_in, ln_gain, ln_bias, qkv_weight, q_bias, v_bias, out_weight, out_bias, pattern, drop_flags
):
    me = lax.axis_index("tm")
    zh, y = me // 4, me % 4
    resid = resid_in[0]
    dp = lax.axis_index("dp")
    x, zl = dp // 4, dp % 4
    pos = jnp.stack([y, x, zh % 2]).astype(jnp.int32)
    goal = ((me + 1 + pattern[0]) % 16).astype(jnp.int32).reshape(12)
    normed = normalise(goal, resid, ln_gain, ln_bias)
    parts, plane, normed = gather_weights(qkv_weight, out_weight, pos, y, zl, normed)
    rows = z_exchange(normed)
    keep = (1 - drop_flags[0]).astype(F32) / (1.0 - DROP_RATE)
    small = other(jnp.concatenate([out_bias[0], keep]))
    rows, small = lax.optimization_barrier((rows, small))
    bias = jnp.concatenate([q_bias[0], jnp.zeros((704,), F32), v_bias[0]])
    bias = jnp.pad(bias.reshape(4, 4, 3, UNIT), ((0, 0), (0, 0), (0, 0), (0, PAD - UNIT)))
    bias = jnp.pad(bias.transpose(2, 0, 1, 3), ((0, 1), (0, 0), (0, 0), (0, 0)))[..., None]
    packed = project(pos, rows, parts, plane, bias)
    heads = lax.all_to_all(packed, "tm", 0, 0, axis_index_groups=Y_GROUPS, tiled=True)
    weights = collect(pos, parts, plane)
    mixed = attend(heads)
    home = lax.all_to_all(mixed, "tm", 0, 0, tiled=True)
    far_resid, far_weights = other(resid), other(weights)
    received = finish(small[1408:], other(home), far_weights, far_resid, small[None, :1408])
    return received[None]


def solution(mesh):
    return jax.shard_map(
        body,
        mesh=mesh,
        in_specs=(
            P("pipe", "dp", "tm", None),
            P("pipe", None),
            P("pipe", None),
            P("pipe", None, "dp"),
            P("pipe", None),
            P("pipe", None),
            P("pipe", None, "dp"),
            P("pipe", None),
            P("tm", "dp", None),
            P("pipe", "dp"),
        ),
        out_specs=P("pipe", "dp", "tm", None),
        check_vma=False,
    )
```

```python
import functools

import jax
import jax.numpy as jnp
from jax import lax
from jax.experimental import pallas as pl
from jax.experimental.pallas import tpu as pltpu
from jax.sharding import PartitionSpec as P

HEAD_DIM = 88
DROP_RATE = 0.25
UNIT = 44
PAD = 48
BF = jnp.bfloat16
F32 = jnp.float32

Z_GROUPS = [[4 * zh + y for zh in range(4)] for y in range(4)]
Y_GROUPS = [[4 * zh + y for y in range(4)] for zh in range(4)]


def params(limit=56 << 20):
    return pltpu.CompilerParams(vmem_limit_bytes=limit)


def norm_kernel(goal_ref, a_ref, b_ref, gain_ref, bias_ref, out_ref):
    z = pl.program_id(0)
    for k, src in enumerate((a_ref, b_ref)):
        rows = src[0]
        mean = jnp.mean(rows, axis=1, keepdims=True)
        centred = rows - mean
        spread = jnp.mean(centred * centred, axis=1, keepdims=True)
        out_ref[0, 64 * k : 64 * k + 64] = (
            centred * lax.rsqrt(spread + 1e-06) * gain_ref[...] + bias_ref[...]
        ).astype(BF)
    row = lax.broadcasted_iota(jnp.int32, (8, 1408), 0)
    tail = jnp.zeros((8, 1408), jnp.int32)
    for k in range(4):
        clip = z if k < 2 else 4 + z // 2
        tail = jnp.where(row == k, goal_ref[2 * clip + k % 2], tail)
    out_ref[0, 128:136] = tail.astype(F32).astype(BF)


def normalise(goal, resid, gain, bias):
    block = (1, 64, 1408)
    return pl.pallas_call(
        norm_kernel,
        grid_spec=pltpu.PrefetchScalarGridSpec(
            num_scalar_prefetch=1,
            grid=(4,),
            in_specs=[
                pl.BlockSpec(block, lambda z, s: (z, 0, 0)),
                pl.BlockSpec(block, lambda z, s: (4 + z // 2, 0, 0)),
                pl.BlockSpec((1, 1408), lambda z, s: (0, 0)),
                pl.BlockSpec((1, 1408), lambda z, s: (0, 0)),
            ],
            out_specs=pl.BlockSpec((1, 136, 1408), lambda z, s: (z, 0, 0)),
        ),
        out_shape=jax.ShapeDtypeStruct((4, 136, 1408), BF),
        compiler_params=params(),
        name="norm",
    )(goal, resid, resid, gain, bias)


VM = pl.BlockSpec(memory_space=pltpu.VMEM)
SM = pl.BlockSpec(memory_space=pltpu.SMEM)


def gather_rows(x_ref, xs):
    for src in range(4):
        for k in range(2):
            at = 256 * k + 64 * src
            xs[at : at + 64] = x_ref[src, 64 * k : 64 * k + 64]


def apply_piece(weights, bias, xs, acc, place):
    got = lax.dot_general(weights, xs[...], (((1,), (1,)), ((), ())), preferred_element_type=F32)
    got = (got + bias).astype(BF)
    for u in range(weights.shape[0] // PAD):
        acc[place(u)] = got[PAD * u : PAD * u + PAD]


def apply_y(w_ref, bias_ref, ys, x0, nx, xs, acc):
    @pl.when(ys < 3)
    def _():
        bias = bias_ref[ys, x0 : x0 + nx, 0:2].reshape(nx * 2 * PAD, 1)
        apply_piece(
            w_ref[...].reshape(nx * 2 * PAD, 1408), bias, xs, acc,
            lambda u: 3 * (4 * (x0 + u // 2) + u % 2) + ys,
        )


def apply_x(w_ref, bias_ref, at, y0, ny, xs, acc):
    bias = bias_ref[y0 : y0 + ny, at, 2:4].reshape(ny * 2 * PAD, 1)
    apply_piece(
        w_ref[0:ny].reshape(ny * 2 * PAD, 1408), bias, xs, acc,
        lambda u: 3 * (4 * at + 2 + u % 2) + y0 + u // 2,
    )


def qkv_kernel(pos_ref, x_ref, a0, a1, a2, a3, a4, b0, b1, b2, b3, b4, bias_ref, out_ref, acc, xs):
    y, x, par = pos_ref[0], pos_ref[1], pos_ref[2]
    gather_rows(x_ref, xs)
    for w_ref, r, first, count in ((a0, 0, 0, 4), (a1, 1, 0, 4), (a2, 3, 0, 4), (a3, 2, 0, 2), (a4, 2, 2, 2)):
        apply_y(w_ref, bias_ref, (y + r) % 4, first, count, xs, acc)
    for w_ref, r, first, count in ((b0, 0, 0, 3), (b1, 1, 0, 3), (b2, 3, 0, 3), (b3, 2, 0, 2), (b4, 2, 2, 1)):
        apply_x(w_ref, bias_ref, (x + r) % 4, first, count, xs, acc)
    meta = jnp.concatenate([x_ref[src, 128:136, 0:64].astype(F32) for src in range(4)], axis=1)
    meta = jnp.concatenate([meta, jnp.zeros_like(meta)], axis=0).astype(BF)
    for y in range(4):
        for j in range(2):
            for g in range(3):
                for k in range(2):
                    row = j * 288 + g * 96 + k * PAD
                    out_ref[y, row : row + PAD, :] = acc[16 * g + 4 * y + 2 * j + k, :, 0:256]
        for g in range(3):
            for k in range(2):
                row = 576 + g * 96 + k * PAD
                out_ref[y, row : row + PAD, :] = acc[16 * g + 4 * y + 2 * par + k, :, 256:512]
        out_ref[y, 864:880, :] = meta


def project(pos, x, pieces, bias):
    return pl.pallas_call(
        qkv_kernel,
        in_specs=[SM] + [VM] * 12,
        out_specs=VM,
        scratch_shapes=[pltpu.VMEM((48, PAD, 512), BF), pltpu.VMEM((512, 1408), BF)],
        out_shape=jax.ShapeDtypeStruct((4, 880, 256), BF),
        compiler_params=params(),
        name="qkv",
    )(pos, x, *pieces, bias)


def order_kernel(pos_ref, *refs):
    for side in range(2):
        out_ref = refs[8 + side]
        for r in range(4):
            out_ref[(pos_ref[1 - side] + r) % 4] = refs[4 * side + r][...]


def order(pos, parts):
    return pl.pallas_call(
        order_kernel,
        in_specs=[SM] + [VM] * 8,
        out_specs=[VM, VM],
        out_shape=[jax.ShapeDtypeStruct((4, 2, PAD, 1408), BF)] * 2,
        compiler_params=params(),
        name="order",
    )(pos, *parts)


def collect_kernel(pos_ref, *refs):
    w_refs, out_ref = refs[:10], refs[10]
    y, x = pos_ref[0], pos_ref[1]
    for w_ref, r, x0, nx in ((w_refs[0], 0, 0, 4), (w_refs[1], 1, 0, 4), (w_refs[2], 3, 0, 4),
                             (w_refs[3], 2, 0, 2), (w_refs[4], 2, 2, 2)):

        @pl.when((y + r) % 4 == 3)
        def _():
            out_ref[x0 : x0 + nx, 0:2] = w_ref[...]

    for w_ref, r, at in ((w_refs[5], 0, 3), (w_refs[6], 1, 3), (w_refs[7], 3, 3), (w_refs[9], 2, 1)):
        out_ref[(x + r) % 4, 2:4] = w_ref[at]


def collect(pos, pieces):
    return pl.pallas_call(
        collect_kernel,
        in_specs=[SM] + [VM] * 10,
        out_specs=VM,
        out_shape=jax.ShapeDtypeStruct((4, 4, PAD, 1408), BF),
        compiler_params=params(),
        name="collect",
    )(pos, *pieces)


def attend_kernel(r_ref, out_ref, ot):
    scale = HEAD_DIM**-0.5
    lane_block = lax.broadcasted_iota(jnp.int32, (1, 256), 1) // 64
    for j in range(3):
        base = 288 * j
        row = 864 + (0 if j < 2 else 2)
        keys = [r_ref[yk, base + 96 : base + 192, :].astype(F32).T.astype(BF) for yk in range(4)]
        for yq in range(4):
            meta = r_ref[yq, 864:880, :].astype(F32)
            first = meta[row - 864 : row - 863, :].astype(jnp.int32)
            second = meta[row - 863 : row - 862, :].astype(jnp.int32)
            own = lane_block * 4 + yq
            queries = r_ref[yq, base : base + 96, :]
            total = jnp.zeros((1, 256), F32)
            mixed = jnp.zeros((96, 256), F32)
            for yk in range(4):
                scores = jnp.dot(keys[yk], queries, preferred_element_type=F32) * scale
                parts = []
                for zk in range(4):
                    block = zk * 4 + yk
                    seen = (first == block) | (second == block) | (own == block)
                    shift = jnp.where(seen, 0.0, -1e30)
                    parts.append(jnp.exp(scores[64 * zk : 64 * zk + 64, :] + shift))
                weights = jnp.concatenate(parts, axis=0)
                total = total + jnp.sum(weights, axis=0, keepdims=True)
                mixed = mixed + jnp.dot(
                    r_ref[yk, base + 192 : base + 288, :],
                    weights.astype(BF),
                    preferred_element_type=F32,
                )
            ot[j * 96 : j * 96 + 96, yq * 256 : yq * 256 + 256] = (mixed / total).astype(BF)
    for yq in range(4):
        for half in range(2):
            at = yq * 256 + half * 128
            low = ot[0:144, at : at + 128]
            high = ot[144:288, at : at + 128]
            out_ref[4 * (2 * half) + yq] = jnp.concatenate([low[:, :64], high[:, :64]], axis=1)
            out_ref[4 * (2 * half + 1) + yq] = jnp.concatenate([low[:, 64:], high[:, 64:]], axis=1)


def attend(r):
    return pl.pallas_call(
        attend_kernel,
        out_shape=jax.ShapeDtypeStruct((16, 144, 128), BF),
        in_specs=[pl.BlockSpec(memory_space=pltpu.VMEM)],
        out_specs=pl.BlockSpec(memory_space=pltpu.VMEM),
        scratch_shapes=[pltpu.VMEM((288, 1024), BF)],
        compiler_params=params(),
        name="attend",
    )(r)


def clip_rows(r_ref, clip):
    pieces = []
    for y in range(4):
        if clip < 4:
            t = 4 * clip + y
            pieces += [r_ref[t, :, 0:64], r_ref[t, 0:48, 64:128]]
        else:
            for odd in range(2):
                t = 4 * (2 * (clip - 4) + odd) + y
                pieces.append(r_ref[t, 48:144, 64:128])
    return jnp.concatenate(pieces, axis=0)


def out_kernel(keep_ref, r_ref, w_ref, resid_ref, bias_ref, out_ref):
    weights = w_ref[...].reshape(768, 1408)
    for pair in range(3):
        rows = jnp.concatenate([clip_rows(r_ref, 2 * pair), clip_rows(r_ref, 2 * pair + 1)], axis=1)
        rows = rows.astype(F32).T.astype(BF)
        branch = jnp.dot(rows, weights, preferred_element_type=F32) + bias_ref[...]
        for k in range(2):
            clip = 2 * pair + k
            out_ref[clip] = resid_ref[clip] + branch[64 * k : 64 * k + 64] * keep_ref[clip]


def finish(keep, r, w, resid, bias):
    return pl.pallas_call(
        out_kernel,
        grid_spec=pltpu.PrefetchScalarGridSpec(
            num_scalar_prefetch=1,
            grid=(1,),
            in_specs=[
                pl.BlockSpec((16, 144, 128), lambda i, s: (0, 0, 0)),
                pl.BlockSpec((4, 4, PAD, 1408), lambda i, s: (0, 0, 0, 0)),
                pl.BlockSpec((6, 64, 1408), lambda i, s: (0, 0, 0)),
                pl.BlockSpec((1, 1408), lambda i, s: (0, 0)),
            ],
            out_specs=pl.BlockSpec((6, 64, 1408), lambda i, s: (0, 0, 0)),
        ),
        out_shape=jax.ShapeDtypeStruct((6, 64, 1408), F32),
        compiler_params=params(),
        name="finish",
    )(keep, r, w, resid, bias)


def z_exchange(x):
    return lax.all_to_all(x, "tm", 0, 0, axis_index_groups=Z_GROUPS, tiled=True)


def ring_perm(kind, by):
    pairs = []
    for z in range(16):
        for y in range(4):
            for x in range(4):
                to = {
                    "x": (z, y, (x + by) % 4),
                    "y": (z, (y + by) % 4, x),
                    "z": ((z + by) % 16, y, x),
                }[kind]
                flat = [(4 * (c // 4) + b) * 16 + 4 * a + c % 4 for c, b, a in ((z, y, x), to)]
                pairs.append(tuple(flat))
    return pairs


def shift(v, kind, by):
    return lax.ppermute(v, ("tm", "dp"), ring_perm(kind, by))


def in_order(rel, at):
    return lax.dynamic_slice_in_dim(jnp.concatenate([rel, rel]), 4 - at, 4, axis=0)


def ring(v, kind):
    half = v.shape[0] // 2
    before = shift(v, kind, 1)
    after = shift(v, kind, -1)
    far_low = shift(before[:half], kind, 1)
    far_high = shift(after[half:], kind, -1)
    return v, after, before, far_low, far_high


def spread(v, kind):
    return v, shift(v, kind, -1), shift(v, kind, 2), shift(v, kind, 1)


def other(v):
    return lax.ppermute(v, "pipe", [(0, 1), (1, 0)])


def gather_weights(qkv_weight, out_weight, pos, y, zl, tie):
    rows = jnp.concatenate([qkv_weight[0].T, out_weight[0].T], axis=0)
    quarter = lax.dynamic_slice(rows, (UNIT * y, 0), (UNIT, 1408))
    quarter = jnp.pad(quarter, ((0, PAD - UNIT), (0, 0)))
    rel = [quarter] + [shift(quarter, "z", by) for by in (-1, -2, 1)]
    *rel, tie = lax.optimization_barrier((*rel, tie))
    line = in_order(jnp.stack(rel), zl)
    by_x, by_y = order(pos, spread(line[:2], "x") + spread(line[2:], "y"))
    return ring(by_x, "y") + ring(by_y, "x"), tie


def body(
    resid_in, ln_gain, ln_bias, qkv_weight, q_bias, v_bias, out_weight, out_bias, pattern, drop_flags
):
    me = lax.axis_index("tm")
    zh, y = me // 4, me % 4
    resid = resid_in[0]
    dp = lax.axis_index("dp")
    x, zl = dp // 4, dp % 4
    pos = jnp.stack([y, x, zh % 2]).astype(jnp.int32)
    goal = ((me + 1 + pattern[0]) % 16).astype(jnp.int32).reshape(12)
    normed = normalise(goal, resid, ln_gain, ln_bias)
    pieces, normed = gather_weights(qkv_weight, out_weight, pos, y, zl, normed)
    rows = z_exchange(normed)
    keep = (1 - drop_flags[0]).astype(F32) / (1.0 - DROP_RATE)
    small = other(jnp.concatenate([out_bias[0], keep]))
    bias = jnp.concatenate([q_bias[0], jnp.zeros((704,), F32), v_bias[0]])
    bias = jnp.pad(bias.reshape(4, 4, 3, UNIT), ((0, 0), (0, 0), (0, 0), (0, PAD - UNIT)))
    bias = bias.transpose(2, 0, 1, 3)[..., None]
    packed = project(pos, rows, pieces, bias)
    weights = collect(pos, pieces)
    heads = lax.all_to_all(packed, "tm", 0, 0, axis_index_groups=Y_GROUPS, tiled=True)
    mixed = attend(heads)
    home = lax.all_to_all(mixed, "tm", 0, 0, tiled=True)
    home, small = lax.optimization_barrier((home, small))
    far_resid, far_weights = other(resid), other(weights)
    received = finish(small[1408:], other(home), far_weights, far_resid, small[None, :1408])
    return received[None]


def solution(mesh):
    return jax.shard_map(
        body,
        mesh=mesh,
        in_specs=(
            P("pipe", "dp", "tm", None),
            P("pipe", None),
            P("pipe", None),
            P("pipe", None, "dp"),
            P("pipe", None),
            P("pipe", None),
            P("pipe", None, "dp"),
            P("pipe", None),
            P("tm", "dp", None),
            P("pipe", "dp"),
        ),
        out_specs=P("pipe", "dp", "tm", None),
        check_vma=False,
    )
```

```python
import functools

import jax
import jax.numpy as jnp
from jax import lax
from jax.experimental import pallas as pl
from jax.experimental.pallas import tpu as pltpu
from jax.sharding import PartitionSpec as P

HEAD_DIM = 88
DROP_RATE = 0.25
UNIT = 44
PAD = 48
BF = jnp.bfloat16
F32 = jnp.float32

Z_GROUPS = [[4 * zh + y for zh in range(4)] for y in range(4)]
Y_GROUPS = [[4 * zh + y for y in range(4)] for zh in range(4)]


def params(limit=56 << 20):
    return pltpu.CompilerParams(vmem_limit_bytes=limit)


def norm_kernel(goal_ref, a_ref, b_ref, gain_ref, bias_ref, out_ref):
    z = pl.program_id(0)
    for k, src in enumerate((a_ref, b_ref)):
        rows = src[0]
        mean = jnp.mean(rows, axis=1, keepdims=True)
        centred = rows - mean
        spread = jnp.mean(centred * centred, axis=1, keepdims=True)
        out_ref[0, 64 * k : 64 * k + 64] = (
            centred * lax.rsqrt(spread + 1e-06) * gain_ref[...] + bias_ref[...]
        ).astype(BF)
    row = lax.broadcasted_iota(jnp.int32, (8, 1408), 0)
    tail = jnp.zeros((8, 1408), jnp.int32)
    for k in range(4):
        clip = z if k < 2 else 4 + z // 2
        tail = jnp.where(row == k, goal_ref[2 * clip + k % 2], tail)
    out_ref[0, 128:136] = tail.astype(F32).astype(BF)


def normalise(goal, resid, gain, bias):
    block = (1, 64, 1408)
    return pl.pallas_call(
        norm_kernel,
        grid_spec=pltpu.PrefetchScalarGridSpec(
            num_scalar_prefetch=1,
            grid=(4,),
            in_specs=[
                pl.BlockSpec(block, lambda z, s: (z, 0, 0)),
                pl.BlockSpec(block, lambda z, s: (4 + z // 2, 0, 0)),
                pl.BlockSpec((1, 1408), lambda z, s: (0, 0)),
                pl.BlockSpec((1, 1408), lambda z, s: (0, 0)),
            ],
            out_specs=pl.BlockSpec((1, 136, 1408), lambda z, s: (z, 0, 0)),
        ),
        out_shape=jax.ShapeDtypeStruct((4, 136, 1408), BF),
        compiler_params=params(),
        name="norm",
    )(goal, resid, resid, gain, bias)


VM = pl.BlockSpec(memory_space=pltpu.VMEM)
SM = pl.BlockSpec(memory_space=pltpu.SMEM)


def gather_rows(x_ref, xs):
    for src in range(4):
        for k in range(2):
            at = 256 * k + 64 * src
            xs[at : at + 64] = x_ref[src, 64 * k : 64 * k + 64]


def apply_piece(weights, bias, xs, acc, place):
    got = lax.dot_general(weights, xs[...], (((1,), (1,)), ((), ())), preferred_element_type=F32)
    got = (got + bias).astype(BF)
    for u in range(weights.shape[0] // PAD):
        acc[place(u)] = got[PAD * u : PAD * u + PAD]


def apply_y(low, high, bias_ref, ys, xs, acc):
    @pl.when(ys < 3)
    def _():
        weights = jnp.concatenate([w[...].reshape(4 * PAD, 1408) for w in (low, high)], axis=0)
        bias = bias_ref[ys, 0:4, 0:2].reshape(8 * PAD, 1)
        apply_piece(weights, bias, xs, acc, lambda u: 3 * (4 * (u // 2) + u % 2) + ys)


def apply_x(low, high, bias_ref, at, xs, acc):
    weights = jnp.concatenate(
        [low[...].reshape(4 * PAD, 1408), high[0:1].reshape(2 * PAD, 1408)], axis=0
    )
    bias = bias_ref[0:3, at, 2:4].reshape(6 * PAD, 1)
    apply_piece(weights, bias, xs, acc, lambda u: 3 * (4 * at + 2 + u % 2) + u // 2)


def qkv_kernel(pos_ref, x_ref, *refs):
    w_refs, (bias_ref, out_ref, acc, xs) = refs[:16], refs[16:]
    y, x, par = pos_ref[0], pos_ref[1], pos_ref[2]
    gather_rows(x_ref, xs)
    for k, r in enumerate((0, 1, 3, 2)):
        apply_y(w_refs[2 * k], w_refs[2 * k + 1], bias_ref, (y + r) % 4, xs, acc)
        apply_x(w_refs[8 + 2 * k], w_refs[9 + 2 * k], bias_ref, (x + r) % 4, xs, acc)
    meta = jnp.concatenate([x_ref[src, 128:136, 0:64].astype(F32) for src in range(4)], axis=1)
    meta = jnp.concatenate([meta, jnp.zeros_like(meta)], axis=0).astype(BF)
    for y in range(4):
        for j in range(2):
            for g in range(3):
                for k in range(2):
                    row = j * 288 + g * 96 + k * PAD
                    out_ref[y, row : row + PAD, :] = acc[16 * g + 4 * y + 2 * j + k, :, 0:256]
        for g in range(3):
            for k in range(2):
                row = 576 + g * 96 + k * PAD
                out_ref[y, row : row + PAD, :] = acc[16 * g + 4 * y + 2 * par + k, :, 256:512]
        out_ref[y, 864:880, :] = meta


def project(pos, x, pieces, bias):
    return pl.pallas_call(
        qkv_kernel,
        in_specs=[SM] + [VM] * 18,
        out_specs=VM,
        scratch_shapes=[pltpu.VMEM((48, PAD, 512), BF), pltpu.VMEM((512, 1408), BF)],
        out_shape=jax.ShapeDtypeStruct((4, 880, 256), BF),
        compiler_params=params(),
        name="qkv",
    )(pos, x, *pieces, bias)


def order_kernel(pos_ref, *refs):
    for side in range(2):
        halves = refs[8 + 2 * side : 10 + 2 * side]
        for r in range(4):
            at = (pos_ref[1 - side] + r) % 4
            for k, out_ref in enumerate(halves):

                @pl.when(at // 2 == k)
                def _():
                    out_ref[at % 2] = refs[4 * side + r][...]


def order(pos, parts):
    return pl.pallas_call(
        order_kernel,
        in_specs=[SM] + [VM] * 8,
        out_specs=[VM] * 4,
        out_shape=[jax.ShapeDtypeStruct((2, 2, PAD, 1408), BF)] * 4,
        compiler_params=params(),
        name="order",
    )(pos, *parts)


def collect_kernel(pos_ref, *refs):
    w_refs, out_ref = refs[:16], refs[16]
    y, x = pos_ref[0], pos_ref[1]
    for k, r in enumerate((0, 1, 3, 2)):

        @pl.when((y + r) % 4 == 3)
        def _():
            out_ref[0:2, 0:2] = w_refs[2 * k][...]
            out_ref[2:4, 0:2] = w_refs[2 * k + 1][...]

        out_ref[(x + r) % 4, 2:4] = w_refs[9 + 2 * k][1]


def collect(pos, pieces):
    return pl.pallas_call(
        collect_kernel,
        in_specs=[SM] + [VM] * 16,
        out_specs=VM,
        out_shape=jax.ShapeDtypeStruct((4, 4, PAD, 1408), BF),
        compiler_params=params(),
        name="collect",
    )(pos, *pieces)


def attend_kernel(r_ref, out_ref, ot):
    scale = HEAD_DIM**-0.5
    lane_block = lax.broadcasted_iota(jnp.int32, (1, 256), 1) // 64
    for j in range(3):
        base = 288 * j
        row = 864 + (0 if j < 2 else 2)
        keys = [r_ref[yk, base + 96 : base + 192, :].astype(F32).T.astype(BF) for yk in range(4)]
        for yq in range(4):
            meta = r_ref[yq, 864:880, :].astype(F32)
            first = meta[row - 864 : row - 863, :].astype(jnp.int32)
            second = meta[row - 863 : row - 862, :].astype(jnp.int32)
            own = lane_block * 4 + yq
            queries = r_ref[yq, base : base + 96, :]
            total = jnp.zeros((1, 256), F32)
            mixed = jnp.zeros((96, 256), F32)
            for yk in range(4):
                scores = jnp.dot(keys[yk], queries, preferred_element_type=F32) * scale
                parts = []
                for zk in range(4):
                    block = zk * 4 + yk
                    seen = (first == block) | (second == block) | (own == block)
                    shift = jnp.where(seen, 0.0, -1e30)
                    parts.append(jnp.exp(scores[64 * zk : 64 * zk + 64, :] + shift))
                weights = jnp.concatenate(parts, axis=0)
                total = total + jnp.sum(weights, axis=0, keepdims=True)
                mixed = mixed + jnp.dot(
                    r_ref[yk, base + 192 : base + 288, :],
                    weights.astype(BF),
                    preferred_element_type=F32,
                )
            ot[j * 96 : j * 96 + 96, yq * 256 : yq * 256 + 256] = (mixed / total).astype(BF)
    for yq in range(4):
        for half in range(2):
            at = yq * 256 + half * 128
            low = ot[0:144, at : at + 128]
            high = ot[144:288, at : at + 128]
            out_ref[4 * (2 * half) + yq] = jnp.concatenate([low[:, :64], high[:, :64]], axis=1)
            out_ref[4 * (2 * half + 1) + yq] = jnp.concatenate([low[:, 64:], high[:, 64:]], axis=1)


def attend(r):
    return pl.pallas_call(
        attend_kernel,
        out_shape=jax.ShapeDtypeStruct((16, 144, 128), BF),
        in_specs=[pl.BlockSpec(memory_space=pltpu.VMEM)],
        out_specs=pl.BlockSpec(memory_space=pltpu.VMEM),
        scratch_shapes=[pltpu.VMEM((288, 1024), BF)],
        compiler_params=params(),
        name="attend",
    )(r)


def clip_rows(r_ref, clip):
    pieces = []
    for y in range(4):
        if clip < 4:
            t = 4 * clip + y
            pieces += [r_ref[t, :, 0:64], r_ref[t, 0:48, 64:128]]
        else:
            for odd in range(2):
                t = 4 * (2 * (clip - 4) + odd) + y
                pieces.append(r_ref[t, 48:144, 64:128])
    return jnp.concatenate(pieces, axis=0)


def out_kernel(keep_ref, r_ref, w_ref, resid_ref, bias_ref, out_ref):
    weights = w_ref[...].reshape(768, 1408)
    for pair in range(3):
        rows = jnp.concatenate([clip_rows(r_ref, 2 * pair), clip_rows(r_ref, 2 * pair + 1)], axis=1)
        rows = rows.astype(F32).T.astype(BF)
        branch = jnp.dot(rows, weights, preferred_element_type=F32) + bias_ref[...]
        for k in range(2):
            clip = 2 * pair + k
            out_ref[clip] = resid_ref[clip] + branch[64 * k : 64 * k + 64] * keep_ref[clip]


def finish(keep, r, w, resid, bias):
    return pl.pallas_call(
        out_kernel,
        grid_spec=pltpu.PrefetchScalarGridSpec(
            num_scalar_prefetch=1,
            grid=(1,),
            in_specs=[
                pl.BlockSpec((16, 144, 128), lambda i, s: (0, 0, 0)),
                pl.BlockSpec((4, 4, PAD, 1408), lambda i, s: (0, 0, 0, 0)),
                pl.BlockSpec((6, 64, 1408), lambda i, s: (0, 0, 0)),
                pl.BlockSpec((1, 1408), lambda i, s: (0, 0)),
            ],
            out_specs=pl.BlockSpec((6, 64, 1408), lambda i, s: (0, 0, 0)),
        ),
        out_shape=jax.ShapeDtypeStruct((6, 64, 1408), F32),
        compiler_params=params(),
        name="finish",
    )(keep, r, w, resid, bias)


def z_exchange(x):
    return lax.all_to_all(x, "tm", 0, 0, axis_index_groups=Z_GROUPS, tiled=True)


def ring_perm(kind, by):
    pairs = []
    for z in range(16):
        for y in range(4):
            for x in range(4):
                to = {
                    "x": (z, y, (x + by) % 4),
                    "y": (z, (y + by) % 4, x),
                    "z": ((z + by) % 16, y, x),
                }[kind]
                flat = [(4 * (c // 4) + b) * 16 + 4 * a + c % 4 for c, b, a in ((z, y, x), to)]
                pairs.append(tuple(flat))
    return pairs


def shift(v, kind, by):
    return lax.ppermute(v, ("tm", "dp"), ring_perm(kind, by))


def in_order(rel, at):
    return lax.dynamic_slice_in_dim(jnp.concatenate([rel, rel]), 4 - at, 4, axis=0)


def ring(low, high, kind):
    before_low = shift(low, kind, 1)
    after_high = shift(high, kind, -1)
    before_high = shift(high, kind, 1)
    after_low = shift(low, kind, -1)
    far_low = shift(before_low, kind, 1)
    far_high = shift(after_high, kind, -1)
    return low, high, after_low, after_high, before_low, before_high, far_low, far_high


def spread(v, kind):
    return v, shift(v, kind, -1), shift(v, kind, 2), shift(v, kind, 1)


def other(v):
    return lax.ppermute(v, "pipe", [(0, 1), (1, 0)])


def gather_weights(qkv_weight, out_weight, pos, y, zl, tie):
    rows = jnp.concatenate([qkv_weight[0].T, out_weight[0].T], axis=0)
    quarter = lax.dynamic_slice(rows, (UNIT * y, 0), (UNIT, 1408))
    quarter = jnp.pad(quarter, ((0, PAD - UNIT), (0, 0)))
    rel = [quarter] + [shift(quarter, "z", by) for by in (-1, -2, 1)]
    *rel, tie = lax.optimization_barrier((*rel, tie))
    line = in_order(jnp.stack(rel), zl)
    x_low, x_high, y_low, y_high = order(pos, spread(line[:2], "x") + spread(line[2:], "y"))
    return ring(x_low, x_high, "y") + ring(y_low, y_high, "x"), tie


def body(
    resid_in, ln_gain, ln_bias, qkv_weight, q_bias, v_bias, out_weight, out_bias, pattern, drop_flags
):
    me = lax.axis_index("tm")
    zh, y = me // 4, me % 4
    resid = resid_in[0]
    dp = lax.axis_index("dp")
    x, zl = dp // 4, dp % 4
    pos = jnp.stack([y, x, zh % 2]).astype(jnp.int32)
    goal = ((me + 1 + pattern[0]) % 16).astype(jnp.int32).reshape(12)
    normed = normalise(goal, resid, ln_gain, ln_bias)
    pieces, normed = gather_weights(qkv_weight, out_weight, pos, y, zl, normed)
    rows = z_exchange(normed)
    keep = (1 - drop_flags[0]).astype(F32) / (1.0 - DROP_RATE)
    small = other(jnp.concatenate([out_bias[0], keep]))
    bias = jnp.concatenate([q_bias[0], jnp.zeros((704,), F32), v_bias[0]])
    bias = jnp.pad(bias.reshape(4, 4, 3, UNIT), ((0, 0), (0, 0), (0, 0), (0, PAD - UNIT)))
    bias = bias.transpose(2, 0, 1, 3)[..., None]
    packed = project(pos, rows, pieces, bias)
    weights = collect(pos, pieces)
    heads = lax.all_to_all(packed, "tm", 0, 0, axis_index_groups=Y_GROUPS, tiled=True)
    mixed = attend(heads)
    home = lax.all_to_all(mixed, "tm", 0, 0, tiled=True)
    home, small = lax.optimization_barrier((home, small))
    far_resid, far_weights = other(resid), other(weights)
    received = finish(small[1408:], other(home), far_weights, far_resid, small[None, :1408])
    return received[None]


def solution(mesh):
    return jax.shard_map(
        body,
        mesh=mesh,
        in_specs=(
            P("pipe", "dp", "tm", None),
            P("pipe", None),
            P("pipe", None),
            P("pipe", None, "dp"),
            P("pipe", None),
            P("pipe", None),
            P("pipe", None, "dp"),
            P("pipe", None),
            P("tm", "dp", None),
            P("pipe", "dp"),
        ),
        out_specs=P("pipe", "dp", "tm", None),
        check_vma=False,
    )
```

```python
import functools

import jax
import jax.numpy as jnp
from jax import lax
from jax.experimental import pallas as pl
from jax.experimental.pallas import tpu as pltpu
from jax.sharding import PartitionSpec as P

HEAD_DIM = 88
DROP_RATE = 0.25
UNIT = 44
PAD = 48
BF = jnp.bfloat16
F32 = jnp.float32

Z_GROUPS = [[4 * zh + y for zh in range(4)] for y in range(4)]
Y_GROUPS = [[4 * zh + y for y in range(4)] for zh in range(4)]


def params(limit=56 << 20):
    return pltpu.CompilerParams(vmem_limit_bytes=limit)


def norm_kernel(goal_ref, a_ref, b_ref, gain_ref, bias_ref, out_ref):
    z = pl.program_id(0)
    for k, src in enumerate((a_ref, b_ref)):
        rows = src[0]
        mean = jnp.mean(rows, axis=1, keepdims=True)
        centred = rows - mean
        spread = jnp.mean(centred * centred, axis=1, keepdims=True)
        out_ref[0, 64 * k : 64 * k + 64] = (
            centred * lax.rsqrt(spread + 1e-06) * gain_ref[...] + bias_ref[...]
        ).astype(BF)
    row = lax.broadcasted_iota(jnp.int32, (8, 1408), 0)
    tail = jnp.zeros((8, 1408), jnp.int32)
    for k in range(4):
        clip = z if k < 2 else 4 + z // 2
        tail = jnp.where(row == k, goal_ref[2 * clip + k % 2], tail)
    out_ref[0, 128:136] = tail.astype(F32).astype(BF)


def normalise(goal, resid, gain, bias):
    block = (1, 64, 1408)
    return pl.pallas_call(
        norm_kernel,
        grid_spec=pltpu.PrefetchScalarGridSpec(
            num_scalar_prefetch=1,
            grid=(4,),
            in_specs=[
                pl.BlockSpec(block, lambda z, s: (z, 0, 0)),
                pl.BlockSpec(block, lambda z, s: (4 + z // 2, 0, 0)),
                pl.BlockSpec((1, 1408), lambda z, s: (0, 0)),
                pl.BlockSpec((1, 1408), lambda z, s: (0, 0)),
            ],
            out_specs=pl.BlockSpec((1, 136, 1408), lambda z, s: (z, 0, 0)),
        ),
        out_shape=jax.ShapeDtypeStruct((4, 136, 1408), BF),
        compiler_params=params(),
        name="norm",
    )(goal, resid, resid, gain, bias)


VM = pl.BlockSpec(memory_space=pltpu.VMEM)
SM = pl.BlockSpec(memory_space=pltpu.SMEM)


def gather_rows(x_ref, xs):
    for src in range(4):
        for k in range(2):
            at = 256 * k + 64 * src
            xs[at : at + 64] = x_ref[src, 64 * k : 64 * k + 64]


def apply_piece(weights, bias, xs, acc, place):
    got = lax.dot_general(weights, xs[...], (((1,), (1,)), ((), ())), preferred_element_type=F32)
    got = (got + bias).astype(BF)
    for u in range(weights.shape[0] // PAD):
        acc[place(u)] = got[PAD * u : PAD * u + PAD]


def apply_y(low, high, bias_ref, ys, xs, acc):
    @pl.when(ys < 3)
    def _():
        weights = jnp.concatenate([w[...].reshape(4 * PAD, 1408) for w in (low, high)], axis=0)
        bias = bias_ref[ys, 0:4, 0:2].reshape(8 * PAD, 1)
        apply_piece(weights, bias, xs, acc, lambda u: 3 * (4 * (u // 2) + u % 2) + ys)


def apply_x(low, high, bias_ref, at, xs, acc):
    weights = jnp.concatenate(
        [low[...].reshape(4 * PAD, 1408), high[0:1].reshape(2 * PAD, 1408)], axis=0
    )
    bias = bias_ref[0:3, at, 2:4].reshape(6 * PAD, 1)
    apply_piece(weights, bias, xs, acc, lambda u: 3 * (4 * at + 2 + u % 2) + u // 2)


def near_kernel(pos_ref, x_ref, *refs):
    w_refs, (bias_ref, acc, xs) = refs[:12], refs[12:]
    y, x = pos_ref[0], pos_ref[1]
    gather_rows(x_ref, xs)
    for k, r in enumerate((0, 1, 3)):
        apply_y(w_refs[2 * k], w_refs[2 * k + 1], bias_ref, (y + r) % 4, xs, acc)
        apply_x(w_refs[6 + 2 * k], w_refs[7 + 2 * k], bias_ref, (x + r) % 4, xs, acc)

    @pl.when((y + 2) % 4 < 3)
    def _():
        for u in range(8):
            acc[3 * (4 * (u // 2) + u % 2) + (y + 2) % 4] = jnp.zeros((PAD, 512), BF)

    for u in range(6):
        acc[3 * (4 * ((x + 2) % 4) + 2 + u % 2) + u // 2] = jnp.zeros((PAD, 512), BF)


def project_near(pos, x, pieces, bias):
    return pl.pallas_call(
        near_kernel,
        in_specs=[SM] + [VM] * 14,
        out_specs=VM,
        scratch_shapes=[pltpu.VMEM((512, 1408), BF)],
        out_shape=jax.ShapeDtypeStruct((48, PAD, 512), BF),
        compiler_params=params(),
        name="near",
    )(pos, x, *pieces, bias)


def far_kernel(pos_ref, x_ref, near_ref, y_low, y_high, x_low, x_high, bias_ref, out_ref, acc, xs):
    y, x, par = pos_ref[0], pos_ref[1], pos_ref[2]
    gather_rows(x_ref, xs)
    acc[...] = near_ref[...]
    apply_y(y_low, y_high, bias_ref, (y + 2) % 4, xs, acc)
    apply_x(x_low, x_high, bias_ref, (x + 2) % 4, xs, acc)
    meta = jnp.concatenate([x_ref[src, 128:136, 0:64].astype(F32) for src in range(4)], axis=1)
    meta = jnp.concatenate([meta, jnp.zeros_like(meta)], axis=0).astype(BF)
    for y in range(4):
        for j in range(2):
            for g in range(3):
                for k in range(2):
                    row = j * 288 + g * 96 + k * PAD
                    out_ref[y, row : row + PAD, :] = acc[16 * g + 4 * y + 2 * j + k, :, 0:256]
        for g in range(3):
            for k in range(2):
                row = 576 + g * 96 + k * PAD
                out_ref[y, row : row + PAD, :] = acc[16 * g + 4 * y + 2 * par + k, :, 256:512]
        out_ref[y, 864:880, :] = meta


def project_far(pos, x, near, pieces, bias):
    return pl.pallas_call(
        far_kernel,
        in_specs=[SM] + [VM] * 7,
        out_specs=VM,
        scratch_shapes=[pltpu.VMEM((48, PAD, 512), BF), pltpu.VMEM((512, 1408), BF)],
        out_shape=jax.ShapeDtypeStruct((4, 880, 256), BF),
        compiler_params=params(),
        name="far",
    )(pos, x, near, *pieces, bias)


def order_kernel(pos_ref, *refs):
    for side in range(2):
        halves = refs[8 + 2 * side : 10 + 2 * side]
        for r in range(4):
            at = (pos_ref[1 - side] + r) % 4
            for k, out_ref in enumerate(halves):

                @pl.when(at // 2 == k)
                def _():
                    out_ref[at % 2] = refs[4 * side + r][...]


def order(pos, parts):
    return pl.pallas_call(
        order_kernel,
        in_specs=[SM] + [VM] * 8,
        out_specs=[VM] * 4,
        out_shape=[jax.ShapeDtypeStruct((2, 2, PAD, 1408), BF)] * 4,
        compiler_params=params(),
        name="order",
    )(pos, *parts)


def collect_kernel(pos_ref, *refs):
    w_refs, out_ref = refs[:16], refs[16]
    y, x = pos_ref[0], pos_ref[1]
    for k, r in enumerate((0, 1, 3, 2)):

        @pl.when((y + r) % 4 == 3)
        def _():
            out_ref[0:2, 0:2] = w_refs[2 * k][...]
            out_ref[2:4, 0:2] = w_refs[2 * k + 1][...]

        out_ref[(x + r) % 4, 2:4] = w_refs[9 + 2 * k][1]


def collect(pos, pieces):
    return pl.pallas_call(
        collect_kernel,
        in_specs=[SM] + [VM] * 16,
        out_specs=VM,
        out_shape=jax.ShapeDtypeStruct((4, 4, PAD, 1408), BF),
        compiler_params=params(),
        name="collect",
    )(pos, *pieces)


def attend_kernel(r_ref, out_ref, ot):
    scale = HEAD_DIM**-0.5
    lane_block = lax.broadcasted_iota(jnp.int32, (1, 256), 1) // 64
    for j in range(3):
        base = 288 * j
        row = 864 + (0 if j < 2 else 2)
        keys = [r_ref[yk, base + 96 : base + 192, :].astype(F32).T.astype(BF) for yk in range(4)]
        for yq in range(4):
            meta = r_ref[yq, 864:880, :].astype(F32)
            first = meta[row - 864 : row - 863, :].astype(jnp.int32)
            second = meta[row - 863 : row - 862, :].astype(jnp.int32)
            own = lane_block * 4 + yq
            queries = r_ref[yq, base : base + 96, :]
            total = jnp.zeros((1, 256), F32)
            mixed = jnp.zeros((96, 256), F32)
            for yk in range(4):
                scores = jnp.dot(keys[yk], queries, preferred_element_type=F32) * scale
                parts = []
                for zk in range(4):
                    block = zk * 4 + yk
                    seen = (first == block) | (second == block) | (own == block)
                    shift = jnp.where(seen, 0.0, -1e30)
                    parts.append(jnp.exp(scores[64 * zk : 64 * zk + 64, :] + shift))
                weights = jnp.concatenate(parts, axis=0)
                total = total + jnp.sum(weights, axis=0, keepdims=True)
                mixed = mixed + jnp.dot(
                    r_ref[yk, base + 192 : base + 288, :],
                    weights.astype(BF),
                    preferred_element_type=F32,
                )
            ot[j * 96 : j * 96 + 96, yq * 256 : yq * 256 + 256] = (mixed / total).astype(BF)
    for yq in range(4):
        for half in range(2):
            at = yq * 256 + half * 128
            low = ot[0:144, at : at + 128]
            high = ot[144:288, at : at + 128]
            out_ref[4 * (2 * half) + yq] = jnp.concatenate([low[:, :64], high[:, :64]], axis=1)
            out_ref[4 * (2 * half + 1) + yq] = jnp.concatenate([low[:, 64:], high[:, 64:]], axis=1)


def attend(r):
    return pl.pallas_call(
        attend_kernel,
        out_shape=jax.ShapeDtypeStruct((16, 144, 128), BF),
        in_specs=[pl.BlockSpec(memory_space=pltpu.VMEM)],
        out_specs=pl.BlockSpec(memory_space=pltpu.VMEM),
        scratch_shapes=[pltpu.VMEM((288, 1024), BF)],
        compiler_params=params(),
        name="attend",
    )(r)


def clip_rows(r_ref, clip):
    pieces = []
    for y in range(4):
        if clip < 4:
            t = 4 * clip + y
            pieces += [r_ref[t, :, 0:64], r_ref[t, 0:48, 64:128]]
        else:
            for odd in range(2):
                t = 4 * (2 * (clip - 4) + odd) + y
                pieces.append(r_ref[t, 48:144, 64:128])
    return jnp.concatenate(pieces, axis=0)


def out_kernel(keep_ref, r_ref, w_ref, resid_ref, bias_ref, out_ref):
    weights = w_ref[...].reshape(768, 1408)
    for pair in range(3):
        rows = jnp.concatenate([clip_rows(r_ref, 2 * pair), clip_rows(r_ref, 2 * pair + 1)], axis=1)
        rows = rows.astype(F32).T.astype(BF)
        branch = jnp.dot(rows, weights, preferred_element_type=F32) + bias_ref[...]
        for k in range(2):
            clip = 2 * pair + k
            out_ref[clip] = resid_ref[clip] + branch[64 * k : 64 * k + 64] * keep_ref[clip]


def finish(keep, r, w, resid, bias):
    return pl.pallas_call(
        out_kernel,
        grid_spec=pltpu.PrefetchScalarGridSpec(
            num_scalar_prefetch=1,
            grid=(1,),
            in_specs=[
                pl.BlockSpec((16, 144, 128), lambda i, s: (0, 0, 0)),
                pl.BlockSpec((4, 4, PAD, 1408), lambda i, s: (0, 0, 0, 0)),
                pl.BlockSpec((6, 64, 1408), lambda i, s: (0, 0, 0)),
                pl.BlockSpec((1, 1408), lambda i, s: (0, 0)),
            ],
            out_specs=pl.BlockSpec((6, 64, 1408), lambda i, s: (0, 0, 0)),
        ),
        out_shape=jax.ShapeDtypeStruct((6, 64, 1408), F32),
        compiler_params=params(),
        name="finish",
    )(keep, r, w, resid, bias)


def z_exchange(x):
    return lax.all_to_all(x, "tm", 0, 0, axis_index_groups=Z_GROUPS, tiled=True)


def ring_perm(kind, by):
    pairs = []
    for z in range(16):
        for y in range(4):
            for x in range(4):
                to = {
                    "x": (z, y, (x + by) % 4),
                    "y": (z, (y + by) % 4, x),
                    "z": ((z + by) % 16, y, x),
                }[kind]
                flat = [(4 * (c // 4) + b) * 16 + 4 * a + c % 4 for c, b, a in ((z, y, x), to)]
                pairs.append(tuple(flat))
    return pairs


def shift(v, kind, by):
    return lax.ppermute(v, ("tm", "dp"), ring_perm(kind, by))


def in_order(rel, at):
    return lax.dynamic_slice_in_dim(jnp.concatenate([rel, rel]), 4 - at, 4, axis=0)


def ring(low, high, kind):
    before_low = shift(low, kind, 1)
    after_high = shift(high, kind, -1)
    before_high = shift(high, kind, 1)
    after_low = shift(low, kind, -1)
    far_low = shift(before_low, kind, 1)
    far_high = shift(after_high, kind, -1)
    return low, high, after_low, after_high, before_low, before_high, far_low, far_high


def spread(v, kind):
    return v, shift(v, kind, -1), shift(v, kind, 2), shift(v, kind, 1)


def other(v):
    return lax.ppermute(v, "pipe", [(0, 1), (1, 0)])


def gather_weights(qkv_weight, out_weight, pos, y, zl, tie):
    rows = jnp.concatenate([qkv_weight[0].T, out_weight[0].T], axis=0)
    quarter = lax.dynamic_slice(rows, (UNIT * y, 0), (UNIT, 1408))
    quarter = jnp.pad(quarter, ((0, PAD - UNIT), (0, 0)))
    rel = [quarter] + [shift(quarter, "z", by) for by in (-1, -2, 1)]
    *rel, tie = lax.optimization_barrier((*rel, tie))
    line = in_order(jnp.stack(rel), zl)
    x_low, x_high, y_low, y_high = order(pos, spread(line[:2], "x") + spread(line[2:], "y"))
    return ring(x_low, x_high, "y") + ring(y_low, y_high, "x"), tie


def body(
    resid_in, ln_gain, ln_bias, qkv_weight, q_bias, v_bias, out_weight, out_bias, pattern, drop_flags
):
    me = lax.axis_index("tm")
    zh, y = me // 4, me % 4
    resid = resid_in[0]
    dp = lax.axis_index("dp")
    x, zl = dp // 4, dp % 4
    pos = jnp.stack([y, x, zh % 2]).astype(jnp.int32)
    goal = ((me + 1 + pattern[0]) % 16).astype(jnp.int32).reshape(12)
    normed = normalise(goal, resid, ln_gain, ln_bias)
    pieces, normed = gather_weights(qkv_weight, out_weight, pos, y, zl, normed)
    rows = z_exchange(normed)
    keep = (1 - drop_flags[0]).astype(F32) / (1.0 - DROP_RATE)
    small = other(jnp.concatenate([out_bias[0], keep]))
    bias = jnp.concatenate([q_bias[0], jnp.zeros((704,), F32), v_bias[0]])
    bias = jnp.pad(bias.reshape(4, 4, 3, UNIT), ((0, 0), (0, 0), (0, 0), (0, PAD - UNIT)))
    bias = bias.transpose(2, 0, 1, 3)[..., None]
    near = project_near(pos, rows, pieces[0:6] + pieces[8:14], bias)
    packed = project_far(pos, rows, near, pieces[6:8] + pieces[14:16], bias)
    weights = collect(pos, pieces)
    heads = lax.all_to_all(packed, "tm", 0, 0, axis_index_groups=Y_GROUPS, tiled=True)
    mixed = attend(heads)
    home = lax.all_to_all(mixed, "tm", 0, 0, tiled=True)
    home, small = lax.optimization_barrier((home, small))
    far_resid, far_weights = other(resid), other(weights)
    received = finish(small[1408:], other(home), far_weights, far_resid, small[None, :1408])
    return received[None]


def solution(mesh):
    return jax.shard_map(
        body,
        mesh=mesh,
        in_specs=(
            P("pipe", "dp", "tm", None),
            P("pipe", None),
            P("pipe", None),
            P("pipe", None, "dp"),
            P("pipe", None),
            P("pipe", None),
            P("pipe", None, "dp"),
            P("pipe", None),
            P("tm", "dp", None),
            P("pipe", "dp"),
        ),
        out_specs=P("pipe", "dp", "tm", None),
        check_vma=False,
    )
```
